512 devices in a mesh: img: 16 (over x, z_hi), band: 32 (over y, z_lo, core).
Axes of the slice: x: 4, y: 4, z: 16 (z_hi: 4, z_lo: 4; z = z_hi * 4 + z_lo), core: 2. Of those that a mesh axis runs over, the one named last changes fastest.
Arguments:
- latents: bfloat16 [16, 64, 64, 1120], P('img', 'band'), may hold values from -6 to 6
- tangents: bfloat16 [16, 64, 64, 1120], P('img', 'band'), may hold values from -6 to 6
- w_expand: bfloat16 [1120, 5632], P('img', 'band'), may hold values from -0.1875 to 0.1875
- b_expand: bfloat16 [5632], P('band'), may hold values from -3 to 3
- w_depth: bfloat16 [9, 5632], P(None, 'band'), may hold values from -2 to 2
- b_depth: bfloat16 [5632], P('band'), may hold values from -3 to 3
Outputs:
- gated: bfloat16 [16, 64, 64, 2816], P('img', 'band')
- gated_tangent: bfloat16 [16, 64, 64, 2816], P('img', 'band')
The draws below stay inside these ranges and needn't reach their ends.
All inputs are finite; a program needn't handle non-finite values.
Results may differ from the reference program's by a relative error of at most 0.0057.
Values may be sent and summed in bfloat16 or wider, within the bound.
No kernel may reach another device: no remote copies, remote signals or barrier semaphores. Data moves between devices by JAX's collectives and lax.ppermute only.
A program may use at most 64 MiB of HBM per device.

```python
import jax
import jax.numpy as jnp
from jax import lax

C = 1120
H = 2816
COLS = 64
IMAGES = 16
ROWS = 64


def block_levels(stream_key, extent, shards, smallest, largest):
    factor_of = 1.0
    for dim, blocks in shards:
        draws = jax.random.uniform(jax.random.fold_in(jax.random.fold_in(stream_key, 6), dim), (blocks,), jnp.float32, smallest / len(shards), largest / len(shards))
        factor_of = factor_of * jnp.repeat(jnp.exp(draws), extent[dim] // blocks).reshape((-1,) + (1,) * (len(extent) - 1 - dim))
    return factor_of


def normal_values(stream_key, dims, spread, limit, pieces=(), dtype=jnp.bfloat16):
    drawn = spread * jax.random.normal(stream_key, dims, jnp.float32)
    if pieces:
        drawn = drawn * block_levels(stream_key, dims, pieces, -0.22, 0.18)
    return jnp.clip(drawn, -limit, limit).astype(dtype)


def setup_inputs(seed: int = 0) -> dict:
    keys = jax.random.split(jax.random.key(seed), 7)
    return {
        "latents": normal_values(keys[0], (IMAGES, ROWS, COLS, C), 1.0, 6.0, ((0, 16), (1, 32))),
        "tangents": normal_values(keys[1], (IMAGES, ROWS, COLS, C), 1.0, 6.0, ((0, 16), (1, 32))),
        "w_expand": normal_values(keys[2], (C, 2 * H), C ** -0.5, 0.1875, ((0, 16), (1, 32))),
        "b_expand": normal_values(keys[3], (2 * H,), 0.5, 3.0, ((0, 32),)),
        "w_depth": normal_values(keys[4], (9, 2 * H), 9 ** -0.5, 2.0, ((1, 32),)),
        "b_depth": normal_values(keys[5], (2 * H,), 0.5, 3.0, ((0, 32),)),
    }


def tangent_act(primal_pre, tangent_pre):
    sigmoid_v = jax.nn.sigmoid(primal_pre)
    value = primal_pre * sigmoid_v
    slope = sigmoid_v * (1.0 + primal_pre * (1.0 - sigmoid_v))
    return value, slope * tangent_pre


def depthwise(padded, depth_taps, row_count, col_count):
    total = jnp.zeros(padded.shape[:-3] + (row_count, col_count, padded.shape[-1]), jnp.float32)
    for row_off in range(3):
        for col_off in range(3):
            window = padded[..., row_off:row_off + row_count, col_off:col_off + col_count, :].astype(jnp.float32)
            total = total + window * depth_taps[3 * row_off + col_off].astype(jnp.float32)
    return total


def finish(mixed, depth_bias, half):
    primal_mix = mixed[0] + depth_bias.astype(jnp.float32)
    tangent_mix = mixed[1]
    gate_value, gate_tangent = tangent_act(primal_mix[..., half:], tangent_mix[..., half:])
    gated = primal_mix[..., :half] * gate_value
    gated_tangent = tangent_mix[..., :half] * gate_value + primal_mix[..., :half] * gate_tangent
    return gated.astype(jnp.bfloat16), gated_tangent.astype(jnp.bfloat16)


def reference(latents, tangents, w_expand, b_expand, w_depth, b_depth):
    token_count = ROWS * COLS

    def one_image(pair):
        image, image_tangent = pair
        stacked = jnp.concatenate([image.reshape(token_count, C), image_tangent.reshape(token_count, C)], 0)
        pre_act = jnp.dot(stacked, w_expand, preferred_element_type=jnp.float32)
        value, slope_tangent = tangent_act(pre_act[:token_count] + b_expand.astype(jnp.float32), pre_act[token_count:])
        activated = jnp.stack([value.astype(jnp.bfloat16), slope_tangent.astype(jnp.bfloat16)])
        activated = activated.reshape(2, ROWS, COLS, 2 * H)
        padded = jnp.pad(activated, ((0, 0), (1, 1), (1, 1), (0, 0)))
        mixed = depthwise(padded, w_depth, ROWS, COLS)
        return finish(mixed, b_depth, H)

    gated, gated_tangent = lax.map(one_image, (latents, tangents))
    return gated, gated_tangent
```

```python
import jax
import jax.numpy as jnp
from jax import lax
from jax.sharding import PartitionSpec as P


def tangent_act(primal_pre, tangent_pre):
    sigmoid_v = jax.nn.sigmoid(primal_pre)
    value = primal_pre * sigmoid_v
    slope = sigmoid_v * (1.0 + primal_pre * (1.0 - sigmoid_v))
    return (value, slope * tangent_pre)


def depthwise(padded, depth_taps, row_count, col_count):
    total = jnp.zeros(padded.shape[:-3] + (row_count, col_count, padded.shape[-1]), jnp.float32)
    for row_off in range(3):
        for col_off in range(3):
            window = padded[
                ..., row_off : row_off + row_count, col_off : col_off + col_count, :
            ].astype(jnp.float32)
            total = total + window * depth_taps[3 * row_off + col_off].astype(jnp.float32)
    return total


def finish(mixed, depth_bias, half):
    primal_mix = mixed[0] + depth_bias.astype(jnp.float32)
    tangent_mix = mixed[1]
    gate_value, gate_tangent = tangent_act(primal_mix[..., half:], tangent_mix[..., half:])
    gated = primal_mix[..., :half] * gate_value
    gated_tangent = tangent_mix[..., :half] * gate_value + primal_mix[..., :half] * gate_tangent
    return (gated.astype(jnp.bfloat16), gated_tangent.astype(jnp.bfloat16))


def on_device(latents, tangents, w_expand, b_expand, w_depth, b_depth):
    row_count, col_count, channels = latents.shape[1:]
    img_count = lax.axis_size("img")
    band_count = lax.axis_size("band")
    band = lax.axis_index("band")
    both = jnp.stack([latents[0], tangents[0]])
    head, tail = both[:, :1], both[:, -1:]
    above = lax.ppermute(tail, "band", [(i, i + 1) for i in range(band_count - 1)])
    below = lax.ppermute(head, "band", [(i + 1, i) for i in range(band_count - 1)])
    small = jnp.concatenate([w_depth, b_expand[None], b_depth[None]], 0)
    small = jnp.pad(small, ((0, img_count - small.shape[0]), (0, 0)))
    mine = lax.dynamic_slice_in_dim(small, lax.axis_index("img"), 1, 0)
    shard = jnp.concatenate([w_expand, mine], 0)
    sent = jnp.broadcast_to(shard[None], (img_count,) + shard.shape)
    blocks = lax.all_to_all(sent, "img", 0, 0)
    depth_rows = w_expand.shape[0]
    columns = jnp.concatenate(
        [blocks[:, :depth_rows].reshape(channels, -1), blocks[:, depth_rows]], 0
    )
    whole = lax.all_gather(columns, "band", axis=1, tiled=True)
    table = whole[channels:]
    full_width = whole.shape[1]
    span_rows = row_count + 2
    span = jnp.concatenate([above, both, below], 1)
    token_count = span_rows * col_count
    stacked = jnp.pad(span.reshape(2 * token_count, channels), ((0, 0), (0, img_count)))
    pre_act = jnp.dot(stacked, whole, preferred_element_type=jnp.float32)
    value, slope_tangent = tangent_act(
        pre_act[:token_count] + table[9].astype(jnp.float32), pre_act[token_count:]
    )
    row = lax.broadcasted_iota(jnp.int32, (token_count, 1), 0) // col_count
    inside = ((row > 0) | (band > 0)) & ((row < span_rows - 1) | (band < band_count - 1))
    activated = jnp.stack(
        [
            jnp.where(inside, value, 0.0).astype(jnp.bfloat16),
            jnp.where(inside, slope_tangent, 0.0).astype(jnp.bfloat16),
        ]
    ).reshape(2, span_rows, col_count, full_width)
    padded = jnp.pad(activated, ((0, 0), (0, 0), (1, 1), (0, 0)))
    mixed = depthwise(padded, table[:9], row_count, col_count)
    gated, gated_tangent = finish(mixed, table[10], full_width // 2)
    return gated[None], gated_tangent[None]


def solution(mesh):
    placed = (
        P("img", "band", None, None),
        P("img", "band", None, None),
        P("img", "band"),
        P("band"),
        P(None, "band"),
        P("band"),
    )
    return jax.shard_map(
        on_device,
        mesh=mesh,
        in_specs=placed,
        out_specs=(P("img", "band", None, None), P("img", "band", None, None)),
        check_vma=False,
    )
```

```python
import functools

import jax
import jax.numpy as jnp
from jax import lax
from jax.experimental import pallas as pl
from jax.experimental.pallas import tpu as pltpu
from jax.sharding import Mesh
from jax.sharding import PartitionSpec as P


SLOT = 72
HALO_ROWS = 6
OUT_ROWS = 4
COLS = 64


def ring_gather(mine, axis, cut):
    here = lax.axis_index(axis)
    up = [(i, (i + 1) % 4) for i in range(4)]
    down = [((i + 1) % 4, i) for i in range(4)]
    before = lax.ppermute(mine, axis, up)
    after = lax.ppermute(mine, axis, down)
    far_low = lax.ppermute(before[:cut], axis, up)
    far_high = lax.ppermute(after[cut:], axis, down)
    out = jnp.zeros((4,) + mine.shape, mine.dtype)
    put = lambda buf, block, slot, row: lax.dynamic_update_slice(
        buf, block[None], (slot, row) + (0,) * (mine.ndim - 1)
    )
    out = put(out, mine, here, 0)
    out = put(out, before, (here + 3) % 4, 0)
    out = put(out, after, (here + 1) % 4, 0)
    out = put(out, far_low, (here + 2) % 4, 0)
    return put(out, far_high, (here + 2) % 4, cut)


def mix_kernel(edge_ref, x_ref, wv_ref, wg_ref, o_ref, pre_ref, e_ref):
    tokens = HALO_ROWS * COLS
    width = o_ref.shape[-1]
    col = lax.broadcasted_iota(jnp.int32, (COLS, width), 0)
    chunk = wv_ref.shape[-2]
    mixes = []
    for w_ref in (wv_ref, wg_ref):
        w4 = w_ref[...].reshape(4, chunk, width)

        def table(i, w_ref=w_ref):
            row = SLOT * (i % 4) + SLOT - 2
            lead = w_ref.shape[:-2]
            pos = [0] * len(lead)
            pos[lead.index(4)] = i // 4
            return w_ref[tuple(pos) + (pl.ds(row, 1), slice(None))].astype(jnp.float32)

        pre_ref[...] = jnp.dot(
            x_ref[...], w4.reshape(4 * chunk, width), preferred_element_type=jnp.float32
        )
        bias = table(9)
        for r in range(HALO_ROWS):
            p = pre_ref[pl.ds(r * COLS, COLS), :] + bias
            t = pre_ref[pl.ds(tokens + r * COLS, COLS), :]
            s = jax.nn.sigmoid(p)
            value = p * s
            slope = s * (1.0 + p * (1.0 - s)) * t
            for k, e in enumerate((value, slope)):
                e = e.astype(jnp.bfloat16).astype(jnp.float32)
                if r in (0, HALO_ROWS - 1):
                    e = jnp.where(edge_ref[0 if r == 0 else 1] > 0, e, 0.0)
                e_ref[k, 0, r] = jnp.where(col == 0, 0.0, pltpu.roll(e, 1, 0))
                e_ref[k, 1, r] = e
                e_ref[k, 2, r] = jnp.where(col == COLS - 1, 0.0, pltpu.roll(e, COLS - 1, 0))
        taps = [table(i) for i in range(9)]
        depth_bias = table(10)
        rows = []
        for r in range(OUT_ROWS):
            pair = []
            for k in range(2):
                total = None
                for a in range(3):
                    for b in range(3):
                        term = e_ref[k, b, r + a] * taps[3 * a + b]
                        total = term if total is None else total + term
                pair.append(total + depth_bias if k == 0 else total)
            rows.append(pair)
        mixes.append(rows)
    for r in range(OUT_ROWS):
        (vp, vt), (gp, gt) = mixes[0][r], mixes[1][r]
        s = jax.nn.sigmoid(gp)
        gate = gp * s
        gate_t = s * (1.0 + gp * (1.0 - s)) * gt
        o_ref[0, 0, r] = (vp * gate).astype(jnp.bfloat16)
        o_ref[0, 1, r] = (vt * gate + vp * gate_t).astype(jnp.bfloat16)


def mix(edges, tokens, weights, y_dim):
    chunk, width = weights.shape[-2:]
    block = [4, 4, 1, chunk, width]
    block[y_dim] = 1

    def spec(shift):
        def where(i, _):
            y = i // 2 + shift
            return (y, 0, i % 2, 0, 0) if y_dim == 0 else (0, y, i % 2, 0, 0)

        return pl.BlockSpec(tuple(block), where)

    n_tok = tokens.shape[0]
    return pl.pallas_call(
        mix_kernel,
        out_shape=jax.ShapeDtypeStruct((4, 2, OUT_ROWS, COLS, width), jnp.bfloat16),
        grid_spec=pltpu.PrefetchScalarGridSpec(
            num_scalar_prefetch=1,
            grid=(4,),
            in_specs=[
                pl.BlockSpec(tokens.shape, lambda i, _: (0, 0)),
                spec(0),
                spec(2),
            ],
            out_specs=pl.BlockSpec(
                (1, 2, OUT_ROWS, COLS, width), lambda i, _: (i, 0, 0, 0, 0)
            ),
            scratch_shapes=[
                pltpu.VMEM((n_tok, width), jnp.float32),
                pltpu.VMEM((2, 3, HALO_ROWS, COLS, width), jnp.float32),
            ],
        ),
        cost_estimate=pl.CostEstimate(
            flops=2 * n_tok * 4 * chunk * width * 8,
            bytes_accessed=2 * weights.size + 2 * tokens.size,
            transcendentals=n_tok * width * 8,
        ),
    )(edges, tokens, weights, weights)


def on_device(latents, tangents, w_expand, b_expand, w_depth, b_depth):
    channels = latents.shape[-1]
    depth_rows, width = w_expand.shape
    core = lax.axis_index("core")
    chip = lax.axis_index(("y", "zl"))
    small = jnp.concatenate([w_depth, b_expand[None], b_depth[None]], 0)
    small = jnp.pad(small, ((0, 16 - small.shape[0]), (0, 0)))
    table_row = lax.dynamic_slice_in_dim(small, lax.axis_index(("x", "zh")), 1, 0)
    shard = jnp.concatenate(
        [w_expand, table_row, jnp.zeros((SLOT - depth_rows - 1, width), w_expand.dtype)], 0
    )
    sent = jnp.broadcast_to(shard[None], (16,) + shard.shape)
    column = lax.all_to_all(sent, ("zh", "zl"), 0, 0)
    column = column.reshape(4, 4, SLOT, width).transpose(1, 0, 2, 3).reshape(4, 4 * SLOT, width)
    first, second = column[:2], column[2:]
    first = ring_gather(first, "x", 1)
    second = ring_gather(second, "y", 1)
    first = ring_gather(first, "y", 2)
    second = ring_gather(second, "x", 2)

    both = jnp.stack([latents[0], tangents[0]])
    edge = jnp.where(core == 0, both[:, :1], both[:, -1:])
    near = [(2 * q + 1, 2 * q + 2) for q in range(15)]
    beyond = lax.ppermute(edge, ("y", "zl", "core"), near + [(b, a) for a, b in near])
    mine = jnp.concatenate(
        [
            jnp.where(core == 0, beyond, both[:, :1]),
            jnp.where(core == 0, both[:, :1], both[:, 1:]),
            jnp.where(core == 0, both[:, 1:], beyond),
        ],
        1,
    )
    theirs = lax.ppermute(mine, "core", [(0, 1), (1, 0)])
    span = jnp.concatenate(
        [jnp.where(core == 0, mine, theirs), jnp.where(core == 0, theirs, mine)], 1
    )
    tokens = span.reshape(-1, 16, depth_rows)
    tokens = jnp.pad(tokens, ((0, 0), (0, 0), (0, SLOT - depth_rows))).reshape(-1, 16 * SLOT)
    edges = jnp.stack([chip > 0, chip < 15]).astype(jnp.int32)

    done = [mix(edges, tokens, first, 0), mix(edges, tokens, second, 1)]
    out = jnp.stack([d.reshape((2, 2) + d.shape[1:]) for d in done], 1)
    keep = lax.dynamic_slice_in_dim(out, 2 * core, 2, 4)
    give = lax.dynamic_slice_in_dim(out, 2 - 2 * core, 2, 4)
    take = lax.ppermute(give, "core", [(0, 1), (1, 0)])
    pairs = jnp.stack([jnp.where(core == 0, keep, take), jnp.where(core == 0, take, keep)], 3)
    whole = pairs.transpose(4, 5, 6, 0, 1, 2, 3, 7).reshape(2, 1, 2, COLS, 16 * width)
    return whole[0], whole[1]


def solution(mesh):
    split = Mesh(mesh.devices.reshape(4, 4, 4, 4, 2), ("x", "zh", "y", "zl", "core"))
    img, band = ("x", "zh"), ("y", "zl", "core")
    placed = (
        P(img, band, None, None),
        P(img, band, None, None),
        P(img, band),
        P(band),
        P(None, band),
        P(band),
    )
    return jax.shard_map(
        on_device,
        mesh=split,
        in_specs=placed,
        out_specs=(P(img, band, None, None), P(img, band, None, None)),
        check_vma=False,
    )
```

```python
import jax
import jax.numpy as jnp
from jax import lax
from jax.experimental import pallas as pl
from jax.experimental.pallas import tpu as pltpu
from jax.sharding import Mesh
from jax.sharding import PartitionSpec as P


LANES = 128
DEPTH = 70
WIDTH = 176
TAIL = WIDTH - LANES
FOLD = DEPTH // 2
BLOCK = 112
MAIN = 80
SIDE = 48
TABLE = DEPTH + FOLD
HALO_ROWS = 6
OUT_ROWS = 4
COLS = 64
TOKENS = HALO_ROWS * COLS


def ring_pieces(mine, axis):
    up = [(i, (i + 1) % 4) for i in range(4)]
    down = [((i + 1) % 4, i) for i in range(4)]
    cut = mine.shape[0] // 2
    before = lax.ppermute(mine, axis, up)
    after = lax.ppermute(mine, axis, down)
    low = lax.ppermute(before[:cut], axis, up)
    high = lax.ppermute(after[cut:], axis, down)
    return mine, after, low, high, before


def mix_kernel(flag_ref, x_ref, *refs, columns_last):
    pieces, (keep_ref, give_ref), (pre_ref, e_ref, m_ref) = refs[:5], refs[5:7], refs[7:]
    own, after, low, high, before = pieces
    core, swap = flag_ref[2], flag_ref[3]

    def packed(yr, j, zl):
        outer, inner = (yr, j) if columns_last else (j, yr)
        if outer == 2:
            ref, at = (low, inner) if inner < 2 else (high, inner - 2)
        else:
            ref, at = {0: own, 1: after, 3: before}[outer], inner
        return ref, 2 * at + zl

    def part(yr, zl, first, rows):
        chunks = []
        for j in range(4):
            ref, at = packed(yr, j, zl)
            for zh in range(4):
                chunks.append(ref[at, pl.ds(zh * BLOCK + first, rows), :])
        return jnp.concatenate(chunks, 0)

    def both(yr, first, rows):
        return jnp.concatenate([part(yr, 0, first, rows), part(yr, 1, first, rows)], 1)

    lane = lax.broadcasted_iota(jnp.int32, (1, LANES), 1)

    def table(yr, i):
        out = []
        for zl in range(2):
            ref, at = packed(yr, 0, zl)
            base = (i // 3) * BLOCK + TABLE + i % 3
            out.append(
                (
                    ref[at, pl.ds(base, 1), :].astype(jnp.float32),
                    ref[at, pl.ds(base + 3, 1), :].astype(jnp.float32),
                )
            )
        return [out[0][0], out[1][0], jnp.where(lane < TAIL, out[0][1], out[1][1])]

    def products(yr, u):
        n_main, n_side = 16 * MAIN, 16 * SIDE
        wide = jnp.dot(
            x_ref[:, :n_main], both(yr, 0, MAIN), preferred_element_type=jnp.float32
        )
        pre_ref[u, 0] = wide[:, :LANES]
        pre_ref[u, 1] = wide[:, LANES:]
        side = both(yr, MAIN - 16, SIDE)
        a = jnp.dot(
            x_ref[:, n_main : n_main + n_side], side, preferred_element_type=jnp.float32
        )
        b = jnp.dot(x_ref[:, n_main + n_side :], side, preferred_element_type=jnp.float32)
        pre_ref[u, 2] = jnp.where(
            lane < TAIL,
            a[:, :LANES] + pltpu.roll(b[:, :LANES], LANES - TAIL, 1),
            pltpu.roll(a[:, LANES:], TAIL, 1) + b[:, LANES:],
        )

    col = lax.broadcasted_iota(jnp.int32, (COLS, LANES), 0)

    def mixing(yr, u, s):
        bias, depth_bias = table(yr, 9), table(yr, 10)
        taps = [table(yr, i) for i in range(9)]
        for g in range(3):

            def act(r, carry, g=g):
                at = pl.multiple_of(r * COLS, COLS)
                p = pre_ref[u, g, pl.ds(at, COLS), :] + bias[g]
                t = pre_ref[u, g, pl.ds(TOKENS + at, COLS), :]
                sig = jax.nn.sigmoid(p)
                pair = (p * sig, sig * (1.0 + p * (1.0 - sig)) * t)
                last = jnp.where(r == HALO_ROWS - 1, flag_ref[1], 1)
                inside = jnp.where(r == 0, flag_ref[0], last) > 0
                for k in range(2):
                    e = jnp.where(inside, pair[k].astype(jnp.bfloat16).astype(jnp.float32), 0.0)
                    e_ref[g, k, 0, r] = jnp.where(col == 0, 0.0, pltpu.roll(e, 1, 0))
                    e_ref[g, k, 1, r] = e
                    e_ref[g, k, 2, r] = jnp.where(
                        col == COLS - 1, 0.0, pltpu.roll(e, COLS - 1, 0)
                    )
                return carry

            def conv(q, carry, g=g):
                r = (2 * core + q) % OUT_ROWS
                for k in range(2):
                    total = depth_bias[g] if k == 0 else None
                    for a in range(3):
                        for b in range(3):
                            term = e_ref[g, k, b, r + a] * taps[3 * a + b][g]
                            total = term if total is None else total + term
                    m_ref[s, g, k, q] = total
                return carry

            lax.fori_loop(0, HALO_ROWS, act, 0)
            lax.fori_loop(0, OUT_ROWS, conv, 0)

    def gating(pair):
        value = swap if pair == 0 else flag_ref[4]
        slot = flag_ref[5] if pair == 0 else 1 - flag_ref[5]

        def rows(i, carry):
            g, half = i // 2, i % 2
            for to, ref in enumerate((keep_ref, give_ref)):
                q = 2 * to + half
                vp, vt = m_ref[2 * pair + value, g, 0, q], m_ref[2 * pair + value, g, 1, q]
                gp, gt = m_ref[2 * pair + 1 - value, g, 0, q], m_ref[2 * pair + 1 - value, g, 1, q]
                sig = jax.nn.sigmoid(gp)
                gate = gp * sig
                gate_t = sig * (1.0 + gp * (1.0 - sig)) * gt
                ref[slot, g, 0, half] = (vp * gate).astype(jnp.bfloat16)
                ref[slot, g, 1, half] = (vt * gate + vp * gate_t).astype(jnp.bfloat16)
            return carry

        lax.fori_loop(0, 6, rows, 0)

    order = (0, 2, 1, 3)
    products(order[0], 0)
    for i, yr in enumerate(order):
        if i < 3:
            products(order[i + 1], (i + 1) % 2)
        mixing(yr, i % 2, i)
        if i % 2 == 1:
            gating(i // 2)


def mix(flags, tokens, pieces, columns_last):
    out = jax.ShapeDtypeStruct((2, 3, 2, 2, COLS, LANES), jnp.bfloat16)
    whole = pl.BlockSpec(memory_space=pltpu.VMEM)
    return pl.pallas_call(
        lambda *refs: mix_kernel(*refs, columns_last=columns_last),
        out_shape=(out, out),
        in_specs=[pl.BlockSpec(memory_space=pltpu.SMEM)] + [whole] * 6,
        out_specs=(whole, whole),
        scratch_shapes=[
            pltpu.VMEM((2, 3, 2 * TOKENS, LANES), jnp.float32),
            pltpu.VMEM((3, 2, 3, HALO_ROWS, COLS, LANES), jnp.float32),
            pltpu.VMEM((4, 3, 2, OUT_ROWS, COLS, LANES), jnp.float32),
        ],
        cost_estimate=pl.CostEstimate(
            flops=2 * tokens.size * 1024, bytes_accessed=6_000_000, transcendentals=2_000_000
        ),
    )(flags, tokens, *pieces)


def weave_kernel(flag_ref, *refs):
    keep, take, out = refs[:2], refs[2:4], refs[4:]
    mine_first = flag_ref[2] == 0
    lane = lax.broadcasted_iota(jnp.int32, (1, LANES), 1)
    for k in range(2):
        for r in range(2):
            segments = []
            for y in range(2):
                for half in range(2):
                    groups = []
                    for g in range(3):
                        own = keep[half][y, g, k, r].astype(jnp.float32)
                        other = take[half][y, g, k, r].astype(jnp.float32)
                        groups.append(
                            (
                                jnp.where(mine_first, own, other),
                                jnp.where(mine_first, other, own),
                            )
                        )
                    for zl in range(2):
                        for core in range(2):
                            start = WIDTH * (8 * y + 4 * half + 2 * zl + core)
                            segments.append((start, 0, LANES, groups[zl][core]))
                            segments.append((start + LANES, TAIL * zl, TAIL, groups[2][core]))
            for n in range(8 * 2 * WIDTH // LANES):
                tile = None
                for start, first, count, block in segments:
                    lo, hi = start - n * LANES, start + count - n * LANES
                    if hi <= 0 or lo >= LANES:
                        continue
                    shift = (lo - first) % LANES
                    moved = pltpu.roll(block, shift, 1) if shift else block
                    if tile is None:
                        tile = moved
                    else:
                        tile = jnp.where((lane >= lo) & (lane < hi), moved, tile)
                out[k][0, r, :, pl.ds(n * LANES, LANES)] = tile.astype(jnp.bfloat16)


def weave(flags, keep, take):
    out = jax.ShapeDtypeStruct((1, 2, COLS, 16 * WIDTH), jnp.bfloat16)
    whole = pl.BlockSpec(memory_space=pltpu.VMEM)
    return pl.pallas_call(
        weave_kernel,
        out_shape=(out, out),
        in_specs=[pl.BlockSpec(memory_space=pltpu.SMEM)] + [whole] * 4,
        out_specs=(whole, whole),
    )(flags, *keep, *take)


def spread(tokens, x):
    k = lax.broadcasted_iota(jnp.int32, (1, 16 * (MAIN + 2 * SIDE)), 1)
    n_main, n_side = 16 * MAIN, 16 * SIDE
    s = k - n_main
    second = (s >= n_side).astype(jnp.int32)
    s = s - n_side * second
    in_main = k < n_main
    unit = jnp.where(in_main, k // MAIN, s // SIDE)
    row = jnp.where(in_main, k % MAIN, s % SIDE - (DEPTH - MAIN + 16))
    limit = jnp.where(in_main, DEPTH, FOLD)
    source = ((x + unit // 4) % 4) * 4 * DEPTH + (unit % 4) * DEPTH + row + jnp.where(in_main, 0, FOLD * second)
    source = jnp.where((row >= 0) & (row < limit), source, -1)
    channel = lax.broadcasted_iota(jnp.int32, (tokens.shape[1], k.shape[1]), 0)
    chosen = (channel == source).astype(jnp.bfloat16)
    return jnp.dot(tokens, chosen, preferred_element_type=jnp.float32).astype(jnp.bfloat16)


def on_device(latents, tangents, w_expand, b_expand, w_depth, b_depth):
    channels = latents.shape[-1]
    core, x, y = lax.axis_index("core"), lax.axis_index("x"), lax.axis_index("y")
    chip = lax.axis_index(("y", "zl"))
    small = jnp.concatenate([w_depth, b_expand[None], b_depth[None], jnp.zeros_like(b_depth)[None]], 0)
    three = lax.dynamic_slice_in_dim(small, 3 * lax.axis_index("zh"), 3, 0)
    zeros = lambda rows, lanes: jnp.zeros((rows, lanes), w_expand.dtype)
    rest, three_rest = w_expand[:, LANES:], three[:, LANES:]
    gap = LANES - 2 * TAIL
    shard = jnp.concatenate(
        [
            w_expand[:, :LANES],
            jnp.concatenate([rest[:FOLD], rest[FOLD:], zeros(FOLD, gap)], 1),
            three[:, :LANES],
            jnp.concatenate([three_rest, three_rest, zeros(3, gap)], 1),
            zeros(1, LANES),
        ],
        0,
    )
    sent = jnp.broadcast_to(shard[None], (16,) + shard.shape)
    column = lax.all_to_all(sent, ("zh", "zl"), 0, 0)

    edge = jnp.where(
        core == 0,
        jnp.concatenate([latents[:, 0], tangents[:, 0]], 0),
        jnp.concatenate([latents[:, -1], tangents[:, -1]], 0),
    )
    near = [(2 * q + 1, 2 * q + 2) for q in range(15)]
    beyond = lax.ppermute(edge, ("y", "zl", "core"), near + [(b, a) for a, b in near])
    rows = [jnp.concatenate([latents[:, r], tangents[:, r]], 0) for r in range(2)]
    mine = jnp.stack(
        [
            jnp.where(core == 0, beyond, rows[0]),
            jnp.where(core == 0, rows[0], rows[1]),
            jnp.where(core == 0, rows[1], beyond),
        ],
        1,
    )
    theirs = lax.ppermute(mine, "core", [(0, 1), (1, 0)])
    span = jnp.concatenate(
        [jnp.where(core == 0, mine, theirs), jnp.where(core == 0, theirs, mine)], 1
    )
    tokens = spread(span.reshape(2 * TOKENS, channels), x)
    tokens, column = lax.optimization_barrier((tokens, column))

    column = column.reshape(4, 4, BLOCK, LANES).transpose(1, 0, 2, 3).reshape(4, 4 * BLOCK, LANES)
    first = jnp.concatenate(ring_pieces(column[:2], "x"), 0)
    second = jnp.concatenate(ring_pieces(column[2:], "y"), 0)
    first = ring_pieces(first, "y")
    second = ring_pieces(second, "x")

    flags = jnp.stack(
        [
            chip > 0,
            chip < 15,
            core == 1,
            y >= 2,
            (y == 1) | (y == 2),
            y % 2 == 1,
        ]
    ).astype(jnp.int32)
    keep_a, give_a = mix(flags, tokens, first, True)
    keep_b, give_b = mix(flags, tokens, second, False)
    across = [(0, 1), (1, 0)]
    take_a, take_b = lax.ppermute(give_a, "core", across), lax.ppermute(give_b, "core", across)
    return weave(flags, (keep_a, keep_b), (take_a, take_b))


def solution(mesh):
    split = Mesh(mesh.devices.reshape(4, 4, 4, 4, 2), ("x", "zh", "y", "zl", "core"))
    img, band = ("x", "zh"), ("y", "zl", "core")
    placed = (
        P(img, band, None, None),
        P(img, band, None, None),
        P(img, band),
        P(band),
        P(None, band),
        P(band),
    )
    return jax.shard_map(
        on_device,
        mesh=split,
        in_specs=placed,
        out_specs=(P(img, band, None, None), P(img, band, None, None)),
        check_vma=False,
    )
```

```python
import jax
import jax.numpy as jnp
from jax import lax
from jax.experimental import pallas as pl
from jax.experimental.pallas import tpu as pltpu
from jax.sharding import Mesh
from jax.sharding import PartitionSpec as P


LANES = 128
DEPTH = 70
WIDTH = 176
HALF = WIDTH // 2
CORE = 64
REST = HALF - CORE
TAIL = 2 * REST
FOLD = DEPTH // 2
BLOCK = 112
TABLE = DEPTH + FOLD
SPAN = 3
OUT_ROWS = 4
COLS = 64
GROUPS = 6


def ring_pieces(mine, axis):
    up = [(i, (i + 1) % 4) for i in range(4)]
    down = [((i + 1) % 4, i) for i in range(4)]
    cut = mine.shape[0] // 2
    before = lax.ppermute(mine, axis, up)
    after = lax.ppermute(mine, axis, down)
    low = lax.ppermute(before[:cut], axis, up)
    high = lax.ppermute(after[cut:], axis, down)
    return mine, after, low, high, before


def mix_kernel(flag_ref, mine_ref, other_ref, w_ref, table_ref, out_ref, pre_ref, e_ref, m_ref):
    core = flag_ref[2]
    n_part = 2 * SPAN * COLS
    for src, ref in enumerate((mine_ref, other_ref)):
        x = ref[...].reshape(n_part, ref.shape[-1])
        for n in range(GROUPS // 2):
            wide = jnp.dot(
                x, w_ref[:, 2 * n * LANES : 2 * (n + 1) * LANES], preferred_element_type=jnp.float32
            )
            pre_ref[2 * n, pl.ds(src * n_part, n_part), :] = wide[:, :LANES]
            pre_ref[2 * n + 1, pl.ds(src * n_part, n_part), :] = wide[:, LANES:]

    col = lax.broadcasted_iota(jnp.int32, (COLS, LANES), 0)
    lane = lax.broadcasted_iota(jnp.int32, (1, LANES), 1)

    def group(g, carry):
        bias, depth_bias = table_ref[g, pl.ds(9, 1), :], table_ref[g, pl.ds(10, 1), :]
        taps = [table_ref[g, pl.ds(i, 1), :] for i in range(9)]

        def act(r, inner):
            late = r // SPAN
            src = jnp.where(core == 0, late, 1 - late)
            at = pl.multiple_of(src * n_part + (r - SPAN * late) * COLS, COLS)
            p = pre_ref[g, pl.ds(at, COLS), :] + bias
            t = pre_ref[g, pl.ds(at + SPAN * COLS, COLS), :]
            sig = jax.nn.sigmoid(p)
            pair = (p * sig, sig * (1.0 + p * (1.0 - sig)) * t)
            last = jnp.where(r == 2 * SPAN - 1, flag_ref[1], 1)
            inside = jnp.where(r == 0, flag_ref[0], last) > 0
            for k in range(2):
                e = jnp.where(inside, pair[k].astype(jnp.bfloat16).astype(jnp.float32), 0.0)
                e_ref[k, 0, r] = jnp.where(col == 0, 0.0, pltpu.roll(e, 1, 0))
                e_ref[k, 1, r] = e
                e_ref[k, 2, r] = jnp.where(col == COLS - 1, 0.0, pltpu.roll(e, COLS - 1, 0))
            return inner

        def conv(q, inner):
            r = (2 * core + q) % OUT_ROWS
            for k in range(2):
                total = depth_bias if k == 0 else None
                for a in range(3):
                    for b in range(3):
                        term = e_ref[k, b, r + a] * taps[3 * a + b]
                        total = term if total is None else total + term
                m_ref[g, k, q] = total
            return inner

        lax.fori_loop(0, 2 * SPAN, act, 0)
        lax.fori_loop(0, OUT_ROWS, conv, 0)
        return carry

    lax.fori_loop(0, GROUPS, group, 0)

    def gated(q, to, split):
        (vp, gp), (vt, gt) = split(0), split(1)
        sig = jax.nn.sigmoid(gp)
        gate = gp * sig
        gate_t = sig * (1.0 + gp * (1.0 - sig)) * gt
        out_ref[q, to, 0] = (vp * gate).astype(jnp.bfloat16)
        out_ref[q, to, 1] = (vt * gate + vp * gate_t).astype(jnp.bfloat16)

    def rows(q, carry):
        for pair in range(2):

            def split(k, pair=pair):
                a, b = m_ref[2 * pair, k, q], m_ref[2 * pair + 1, k, q]
                value = jnp.where(lane < CORE, a, pltpu.roll(b, CORE, 1))
                return value, jnp.where(lane < CORE, pltpu.roll(a, CORE, 1), b)

            gated(q, pair, split)
        here = (lane < REST) | ((lane >= TAIL) & (lane < TAIL + REST))

        def split_tail(k):
            a, b = m_ref[4, k, q], m_ref[5, k, q]
            value = jnp.where(here, a, pltpu.roll(b, REST, 1))
            return value, jnp.where(here, pltpu.roll(a, LANES - REST, 1), b)

        gated(q, 2, split_tail)
        return carry

    lax.fori_loop(0, OUT_ROWS, rows, 0)


def mix(flags, mine, others, weights, table, slot):
    whole = pl.BlockSpec(memory_space=pltpu.VMEM)
    part = pl.BlockSpec((1,) + mine.shape[1:], lambda i: (slot, 0, 0, 0, 0))
    n_tok = 4 * SPAN * COLS
    return pl.pallas_call(
        mix_kernel,
        grid=(1,),
        out_shape=jax.ShapeDtypeStruct((OUT_ROWS, 3, 2, COLS, LANES), jnp.bfloat16),
        in_specs=[pl.BlockSpec(memory_space=pltpu.SMEM), part, part, whole, whole],
        out_specs=whole,
        scratch_shapes=[
            pltpu.VMEM((GROUPS, n_tok, LANES), jnp.float32),
            pltpu.VMEM((2, 3, 2 * SPAN, COLS, LANES), jnp.float32),
            pltpu.VMEM((GROUPS, 2, OUT_ROWS, COLS, LANES), jnp.float32),
        ],
        cost_estimate=pl.CostEstimate(
            flops=2 * n_tok * weights.size, bytes_accessed=5_000_000, transcendentals=1_000_000
        ),
    )(flags, mine, others, weights, table)


def weave_kernel(flag_ref, keep_ref, take_ref, *out):
    mine_first = flag_ref[0] == 0
    y = flag_ref[1]
    lane = lax.broadcasted_iota(jnp.int32, (1, LANES), 1)

    def row(r, carry):
        for k in range(2):
            segments = []
            for source in range(4):
                at = (source - y + 4) % 4
                groups = []
                for g in range(3):
                    own = keep_ref[at, r, g, k].astype(jnp.float32)
                    other = take_ref[at, r, g, k].astype(jnp.float32)
                    groups.append(
                        (jnp.where(mine_first, own, other), jnp.where(mine_first, other, own))
                    )
                for zl in range(4):
                    for core in range(2):
                        start = WIDTH * (8 * (source % 2) + 2 * zl + core) + HALF * (source // 2)
                        odd, pair = zl % 2, zl // 2
                        segments.append((start, CORE * odd, CORE, groups[pair][core]))
                        lanes = TAIL * odd + REST * pair
                        segments.append((start + CORE, lanes, REST, groups[2][core]))
            for n in range(16 * WIDTH // LANES):
                tile = None
                for start, first, count, block in segments:
                    lo, hi = start - n * LANES, start + count - n * LANES
                    if hi <= 0 or lo >= LANES:
                        continue
                    shift = (lo - first) % LANES
                    moved = pltpu.roll(block, shift, 1) if shift else block
                    if tile is None:
                        tile = moved
                    else:
                        tile = jnp.where((lane >= lo) & (lane < hi), moved, tile)
                out[k][0, r, :, pl.ds(n * LANES, LANES)] = tile.astype(jnp.bfloat16)
        return carry

    lax.fori_loop(0, 2, row, 0)


def weave(flags, keep, take):
    out = jax.ShapeDtypeStruct((1, 2, COLS, 16 * WIDTH), jnp.bfloat16)
    whole = pl.BlockSpec(memory_space=pltpu.VMEM)
    return pl.pallas_call(
        weave_kernel,
        out_shape=(out, out),
        in_specs=[pl.BlockSpec(memory_space=pltpu.SMEM)] + [whole] * 2,
        out_specs=(whole, whole),
    )(flags, keep, take)


def on_device(latents, tangents, w_expand, b_expand, w_depth, b_depth):
    channels = latents.shape[-1]
    core, x, y = lax.axis_index("core"), lax.axis_index("x"), lax.axis_index("y")
    zl = lax.axis_index("zl")
    across = [(0, 1), (1, 0)]
    small = jnp.concatenate([w_depth, b_expand[None], b_depth[None], jnp.zeros_like(b_depth)[None]], 0)
    three = lax.dynamic_slice_in_dim(small, 3 * lax.axis_index("zh"), 3, 0)
    shard = jnp.concatenate([w_expand, three], 0)
    front = y < 2
    low, high = shard[:, :HALF], shard[:, HALF:]
    got = lax.ppermute(jnp.where(front, high, low), "y", [(i, (i + 2) % 4) for i in range(4)])
    held = jnp.where(front, low, high)
    value, gate = jnp.where(front, held, got), jnp.where(front, got, held)
    zeros = lambda rows, lanes: jnp.zeros((rows, lanes), w_expand.dtype)
    main = jnp.concatenate([value[:, :CORE], gate[:, :CORE]], 1)
    tail = jnp.concatenate([value[:, CORE:], gate[:, CORE:]], 1)
    block = jnp.concatenate(
        [
            main[:DEPTH],
            jnp.concatenate([tail[:FOLD], tail[FOLD:DEPTH], zeros(FOLD, LANES - 2 * TAIL)], 1),
            main[DEPTH:],
            jnp.concatenate([tail[DEPTH:], zeros(3, LANES - TAIL)], 1),
            zeros(1, LANES),
        ],
        0,
    )
    sent = jnp.broadcast_to(block[None], (16,) + block.shape)
    column = lax.all_to_all(sent, ("zh", "zl"), 0, 0)

    edge = jnp.where(
        core == 0,
        jnp.concatenate([latents[:, 0], tangents[:, 0]], 0),
        jnp.concatenate([latents[:, -1], tangents[:, -1]], 0),
    )
    near = [(2 * q + 1, 2 * q + 2) for q in range(15)]
    beyond = lax.ppermute(edge, ("y", "zl", "core"), near + [(b, a) for a, b in near])
    rows = [jnp.concatenate([latents[:, r], tangents[:, r]], 0) for r in range(2)]
    mine = jnp.stack(
        [
            jnp.where(core == 0, beyond, rows[0]),
            jnp.where(core == 0, rows[0], rows[1]),
            jnp.where(core == 0, rows[1], beyond),
        ],
        1,
    )
    own, after, low, high, before = ring_pieces(mine, "y")
    mine = jnp.stack([own, after, jnp.concatenate([low, high], 0), before])
    others = lax.ppermute(mine, "core", across)

    own, after, low, high, before = ring_pieces(column, "x")
    turned = jnp.concatenate([own, after, low, high, before], 0).reshape(4, 4, 4, BLOCK, LANES)
    turned = jnp.concatenate([turned, turned[:3]], 0)
    ordered = lax.dynamic_slice_in_dim(turned, (4 - x) % 4, 4, 0).reshape(16, 4, BLOCK, LANES)
    first = ordered[:, :, :DEPTH].transpose(0, 2, 1, 3).reshape(channels, 4 * LANES)
    folded = ordered[:, :, DEPTH:TABLE]
    second = jnp.concatenate([folded[..., :TAIL], folded[..., TAIL : 2 * TAIL]], 2)
    tails = lambda t, n: jnp.pad(
        t.transpose(0, 2, 1, 3).reshape(n, 2, 2 * TAIL), ((0, 0), (0, 0), (0, LANES - 2 * TAIL))
    )
    weights = jnp.concatenate([first, tails(second, channels).reshape(channels, 2 * LANES)], 1)
    extra = ordered[:4, :, TABLE : TABLE + 6]
    table = jnp.concatenate(
        [
            extra[:, :, :3].transpose(0, 2, 1, 3).reshape(12, 4, LANES),
            tails(extra[:, :, 3:, :TAIL], 12),
        ],
        1,
    ).transpose(1, 0, 2).astype(jnp.float32)

    results = {}
    for turn in (2, 1, 3, 0):
        chip = 4 * ((y + turn) % 4) + zl
        flags = jnp.stack([(chip > 0).astype(jnp.int32), (chip < 15).astype(jnp.int32), core])
        done = mix(flags, mine, others, weights, table, turn)
        if turn:
            done = lax.ppermute(done, "y", [(i, (i + turn) % 4) for i in range(4)])
        results[(4 - turn) % 4] = done
    keep = jnp.stack([results[i] for i in range(4)])
    give = jnp.stack([results[i][2:] for i in range(4)])
    take = lax.ppermute(give, "core", across)
    return weave(jnp.stack([core, y]), keep, take)


def solution(mesh):
    split = Mesh(mesh.devices.reshape(4, 4, 4, 4, 2), ("x", "zh", "y", "zl", "core"))
    img, band = ("x", "zh"), ("y", "zl", "core")
    placed = (
        P(img, band, None, None),
        P(img, band, None, None),
        P(img, band),
        P(band),
        P(None, band),
        P(band),
    )

    return jax.shard_map(
        on_device,
        mesh=split,
        in_specs=placed,
        out_specs=(P(img, band, None, None), P(img, band, None, None)),
        check_vma=False,
    )
```

```python
import functools

import jax
import jax.numpy as jnp
from jax import lax
from jax.experimental import pallas as pl
from jax.experimental.pallas import tpu as pltpu
from jax.sharding import Mesh
from jax.sharding import PartitionSpec as P


LANES = 128
DEPTH = 70
WIDTH = 176
HALF = WIDTH // 2
CORE = 64
REST = HALF - CORE
TAIL = 2 * REST
FOLD = DEPTH // 2
TABLE = DEPTH + FOLD
SPAN = 3
OUT_ROWS = 4
COLS = 64
MAIN = 80
SIDE = 48
GROUPS = 6


def ring_pieces(mine, axis):
    up = [(i, (i + 1) % 4) for i in range(4)]
    down = [((i + 1) % 4, i) for i in range(4)]
    cut = mine.shape[0] // 2
    before = lax.ppermute(mine, axis, up)
    after = lax.ppermute(mine, axis, down)
    low = lax.ppermute(before[:cut], axis, up)
    high = lax.ppermute(after[cut:], axis, down)
    return mine, after, low, high, before


def sigmoid(v):
    return 0.5 + 0.5 * jnp.tanh(0.5 * v)


def mix_kernel(flag_ref, *refs, slot):
    parts, (w_ref, table_ref, out_ref, x_ref, pre_ref, e_ref, m_ref) = refs[:4], refs[4:]
    core, first_in, last_in = flag_ref[0], flag_ref[1 + 2 * slot], flag_ref[2 + 2 * slot]
    n_part = 2 * SPAN * COLS
    for i, ref in enumerate(parts):
        x_ref[pl.ds(i * SPAN * COLS, SPAN * COLS), :] = ref[...].reshape(SPAN * COLS, -1)
    for n in range(GROUPS // 2):
        wide = jnp.dot(
            x_ref[...],
            w_ref[:, 2 * n * LANES : 2 * (n + 1) * LANES],
            preferred_element_type=jnp.float32,
        )
        pre_ref[2 * n] = wide[:, :LANES]
        pre_ref[2 * n + 1] = wide[:, LANES:]

    col = lax.broadcasted_iota(jnp.int32, (COLS, LANES), 0)
    lane = lax.broadcasted_iota(jnp.int32, (1, LANES), 1)

    def group(g, carry):
        bias, depth_bias = table_ref[g, pl.ds(9, 1), :], table_ref[g, pl.ds(10, 1), :]
        taps = [table_ref[g, pl.ds(i, 1), :] for i in range(9)]

        def act(r, inner):
            late = r // SPAN
            src = jnp.where(core == 0, late, 1 - late)
            at = pl.multiple_of(src * n_part + (r - SPAN * late) * COLS, COLS)
            p = pre_ref[g, pl.ds(at, COLS), :] + bias
            t = pre_ref[g, pl.ds(at + SPAN * COLS, COLS), :]
            sig = sigmoid(p)
            pair = (p * sig, sig * (1.0 + p * (1.0 - sig)) * t)
            last = jnp.where(r == 2 * SPAN - 1, last_in, 1)
            inside = jnp.where(r == 0, first_in, last) > 0
            for k in range(2):
                e = jnp.where(inside, pair[k].astype(jnp.bfloat16).astype(jnp.float32), 0.0)
                e_ref[k, 0, r] = jnp.where(col == 0, 0.0, pltpu.roll(e, 1, 0))
                e_ref[k, 1, r] = e
                e_ref[k, 2, r] = jnp.where(col == COLS - 1, 0.0, pltpu.roll(e, COLS - 1, 0))
            return inner

        def conv(q, inner):
            r = (2 * core + q) % OUT_ROWS
            for k in range(2):
                total = depth_bias if k == 0 else None
                for a in range(3):
                    for b in range(3):
                        term = e_ref[k, b, r + a] * taps[3 * a + b]
                        total = term if total is None else total + term
                m_ref[g, k, q] = total
            return inner

        lax.fori_loop(0, 2 * SPAN, act, 0)
        lax.fori_loop(0, OUT_ROWS, conv, 0)
        return carry

    lax.fori_loop(0, GROUPS, group, 0)

    def gated(q, to, split):
        (vp, gp), (vt, gt) = split(0), split(1)
        sig = sigmoid(gp)
        gate = gp * sig
        gate_t = sig * (1.0 + gp * (1.0 - sig)) * gt
        out_ref[q, to, 0] = (vp * gate).astype(jnp.bfloat16)
        out_ref[q, to, 1] = (vt * gate + vp * gate_t).astype(jnp.bfloat16)

    def rows(q, carry):
        for pair in range(2):

            def split(k, pair=pair):
                a, b = m_ref[2 * pair, k, q], m_ref[2 * pair + 1, k, q]
                value = jnp.where(lane < CORE, a, pltpu.roll(b, CORE, 1))
                return value, jnp.where(lane < CORE, pltpu.roll(a, CORE, 1), b)

            gated(q, pair, split)
        here = (lane < REST) | ((lane >= TAIL) & (lane < TAIL + REST))

        def split_tail(k):
            a, b = m_ref[4, k, q], m_ref[5, k, q]
            value = jnp.where(here, a, pltpu.roll(b, REST, 1))
            return value, jnp.where(here, pltpu.roll(a, LANES - REST, 1), b)

        gated(q, 2, split_tail)
        return carry

    lax.fori_loop(0, OUT_ROWS, rows, 0)


def mix(flags, parts, weights, table, slot):
    whole = pl.BlockSpec(memory_space=pltpu.VMEM)
    channels = weights.shape[0]

    def part(at):
        return pl.BlockSpec((1, 1, SPAN, COLS, channels), lambda i: (*at, 0, 0, 0))

    n_tok = 4 * SPAN * COLS
    return pl.pallas_call(
        functools.partial(mix_kernel, slot=slot),
        grid=(1,),
        out_shape=jax.ShapeDtypeStruct((OUT_ROWS, 3, 2, COLS, LANES), jnp.bfloat16),
        in_specs=[pl.BlockSpec(memory_space=pltpu.SMEM)] + [part(at) for _, at in parts] + [whole, whole],
        out_specs=whole,
        scratch_shapes=[
            pltpu.VMEM((n_tok, channels), jnp.bfloat16),
            pltpu.VMEM((GROUPS, n_tok, LANES), jnp.float32),
            pltpu.VMEM((2, 3, 2 * SPAN, COLS, LANES), jnp.float32),
            pltpu.VMEM((GROUPS, 2, OUT_ROWS, COLS, LANES), jnp.float32),
        ],
        cost_estimate=pl.CostEstimate(
            flops=2 * n_tok * weights.size, bytes_accessed=5_000_000, transcendentals=1_000_000
        ),
    )(flags, *[array for array, _ in parts], weights, table)


def order_kernel(chosen_ref, own, after, low, high, before, w_ref, table_ref):
    def block(j, zh, zl):
        if j == 2:
            return (low, 4 * zh + zl) if zh < 2 else (high, 4 * (zh - 2) + zl)
        return {0: own, 1: after, 3: before}[j], 4 * zh + zl

    def part(zl, first, rows):
        chunks = []
        for j in range(4):
            for zh in range(4):
                ref, at = block(j, zh, zl)
                chunks.append(ref[at, pl.ds(first, rows), :])
        return jnp.concatenate(chunks, 0)

    lane = lax.broadcasted_iota(jnp.int32, (1, LANES), 1)
    n_main, n_side = 16 * MAIN, 16 * SIDE
    pick = lambda first, count, w: jnp.dot(
        chosen_ref[:, first : first + count], w, preferred_element_type=jnp.float32
    )
    for pair in range(2):
        zls = (2 * pair, 2 * pair + 1)
        main = jnp.concatenate([part(zl, 0, MAIN) for zl in zls], 1)
        side = jnp.concatenate([part(zl, MAIN - 16, SIDE) for zl in zls], 1)
        w_ref[:, 2 * pair * LANES : 2 * (pair + 1) * LANES] = pick(0, n_main, main).astype(jnp.bfloat16)
        a, b = pick(n_main, n_side, side), pick(n_main + n_side, n_side, side)
        even = a[:, :LANES] + pltpu.roll(b[:, :LANES], LANES - TAIL, 1)
        odd = jnp.where(lane < 2 * TAIL, pltpu.roll(a[:, LANES:], TAIL, 1) + b[:, LANES:], 0.0)
        w_ref[:, (4 + pair) * LANES : (5 + pair) * LANES] = jnp.where(lane < TAIL, even, odd).astype(
            jnp.bfloat16
        )
    for i in range(11):
        at, row = 4 * (i // 3), TABLE + i % 3
        line = lambda zl, r: own[at + zl, pl.ds(r, 1), :].astype(jnp.float32)
        for zl in range(4):
            table_ref[zl, pl.ds(i, 1), :] = line(zl, row)
        for pair in range(2):
            odd = jnp.where(lane < 2 * TAIL, pltpu.roll(line(2 * pair + 1, row + 3), TAIL, 1), 0.0)
            table_ref[4 + pair, pl.ds(i, 1), :] = jnp.where(lane < TAIL, line(2 * pair, row + 3), odd)


def in_order(chosen, pieces):
    whole = pl.BlockSpec(memory_space=pltpu.VMEM)
    channels = chosen.shape[0]
    return pl.pallas_call(
        order_kernel,
        out_shape=(
            jax.ShapeDtypeStruct((channels, GROUPS * LANES), jnp.bfloat16),
            jax.ShapeDtypeStruct((GROUPS, 12, LANES), jnp.float32),
        ),
        in_specs=[whole] * 6,
        out_specs=(whole, whole),
        cost_estimate=pl.CostEstimate(
            flops=1024 * chosen.size, bytes_accessed=10_000_000, transcendentals=0
        ),
    )(chosen, *pieces)


def chooser(channels, x):
    n_main, n_side = 16 * MAIN, 16 * SIDE
    k = lax.broadcasted_iota(jnp.int32, (1, n_main + 2 * n_side), 1)
    s = k - n_main
    second = (s >= n_side).astype(jnp.int32)
    s = s - n_side * second
    in_main = k < n_main
    unit = jnp.where(in_main, k // MAIN, s // SIDE)
    row = jnp.where(in_main, k % MAIN, s % SIDE - (DEPTH - MAIN + 16))
    limit = jnp.where(in_main, DEPTH, FOLD)
    source = ((x + unit // 4) % 4) * 4 * DEPTH + (unit % 4) * DEPTH + row
    source = source + jnp.where(in_main, 0, FOLD * second)
    source = jnp.where((row >= 0) & (row < limit), source, -1)
    channel = lax.broadcasted_iota(jnp.int32, (channels, k.shape[1]), 0)
    return (channel == source).astype(jnp.bfloat16)


def weave_kernel(flag_ref, keep_ref, take_ref, *out):
    mine_first = flag_ref[0] == 0
    y = flag_ref[1]
    lane = lax.broadcasted_iota(jnp.int32, (1, LANES), 1)

    def row(r, carry):
        for k in range(2):
            segments = []
            for source in range(4):
                at = (source - y + 4) % 4
                groups = []
                for g in range(3):
                    own = keep_ref[at, r, g, k].astype(jnp.float32)
                    other = take_ref[at, r, g, k].astype(jnp.float32)
                    groups.append(
                        (jnp.where(mine_first, own, other), jnp.where(mine_first, other, own))
                    )
                for zl in range(4):
                    for core in range(2):
                        start = WIDTH * (8 * (source % 2) + 2 * zl + core) + HALF * (source // 2)
                        odd, pair = zl % 2, zl // 2
                        segments.append((start, CORE * odd, CORE, groups[pair][core]))
                        lanes = TAIL * odd + REST * pair
                        segments.append((start + CORE, lanes, REST, groups[2][core]))
            for n in range(16 * WIDTH // LANES):
                tile = None
                for start, first, count, block in segments:
                    lo, hi = start - n * LANES, start + count - n * LANES
                    if hi <= 0 or lo >= LANES:
                        continue
                    shift = (lo - first) % LANES
                    moved = pltpu.roll(block, shift, 1) if shift else block
                    if tile is None:
                        tile = moved
                    else:
                        tile = jnp.where((lane >= lo) & (lane < hi), moved, tile)
                out[k][0, r, :, pl.ds(n * LANES, LANES)] = tile.astype(jnp.bfloat16)
        return carry

    lax.fori_loop(0, 2, row, 0)


def weave(flags, keep, take):
    out = jax.ShapeDtypeStruct((1, 2, COLS, 16 * WIDTH), jnp.bfloat16)
    whole = pl.BlockSpec(memory_space=pltpu.VMEM)
    return pl.pallas_call(
        weave_kernel,
        out_shape=(out, out),
        in_specs=[pl.BlockSpec(memory_space=pltpu.SMEM)] + [whole] * 2,
        out_specs=(whole, whole),
    )(flags, keep, take)


def on_device(latents, tangents, w_expand, b_expand, w_depth, b_depth):
    channels = latents.shape[-1]
    core, x, y = lax.axis_index("core"), lax.axis_index("x"), lax.axis_index("y")
    zl = lax.axis_index("zl")
    across = [(0, 1), (1, 0)]
    small = jnp.concatenate([w_depth, b_expand[None], b_depth[None], jnp.zeros_like(b_depth)[None]], 0)
    three = lax.dynamic_slice_in_dim(small, 3 * lax.axis_index("zh"), 3, 0)
    shard = jnp.concatenate([w_expand, three], 0)
    front = y < 2
    low, high = shard[:, :HALF], shard[:, HALF:]
    got = lax.ppermute(jnp.where(front, high, low), "y", [(i, (i + 2) % 4) for i in range(4)])
    held = jnp.where(front, low, high)
    value, gate = jnp.where(front, held, got), jnp.where(front, got, held)
    zeros = lambda rows, lanes: jnp.zeros((rows, lanes), w_expand.dtype)
    main = jnp.concatenate([value[:, :CORE], gate[:, :CORE]], 1)
    tail = jnp.concatenate([value[:, CORE:], gate[:, CORE:]], 1)
    block = jnp.concatenate(
        [
            main[:DEPTH],
            jnp.concatenate([tail[:FOLD], tail[FOLD:DEPTH], zeros(FOLD, LANES - 2 * TAIL)], 1),
            main[DEPTH:],
            jnp.concatenate([tail[DEPTH:], zeros(3, LANES - TAIL)], 1),
            zeros(1, LANES),
        ],
        0,
    )
    sent = jnp.broadcast_to(block[None], (16,) + block.shape)
    column = lax.all_to_all(sent, ("zh", "zl"), 0, 0)

    edge = jnp.where(
        core == 0,
        jnp.concatenate([latents[:, 0], tangents[:, 0]], 0),
        jnp.concatenate([latents[:, -1], tangents[:, -1]], 0),
    )
    near = [(2 * q + 1, 2 * q + 2) for q in range(15)]
    beyond = lax.ppermute(edge, ("y", "zl", "core"), near + [(b, a) for a, b in near])
    rows = [jnp.concatenate([latents[:, r], tangents[:, r]], 0) for r in range(2)]
    mine = jnp.stack(
        [
            jnp.where(core == 0, beyond, rows[0]),
            jnp.where(core == 0, rows[0], rows[1]),
            jnp.where(core == 0, rows[1], beyond),
        ],
        1,
    )
    own, after, low, high, before = ring_pieces(mine, "y")
    near = jnp.stack([own, after, before])
    low, high = low[None], high[None]
    near_other = lax.ppermute(near, "core", across)
    low_other = lax.ppermute(low, "core", across)
    high_other = lax.ppermute(high, "core", across)
    parts = {
        i: [(near, (at, 0)), (near, (at, 1)), (near_other, (at, 0)), (near_other, (at, 1))]
        for i, at in ((0, 0), (1, 1), (3, 2))
    }
    parts[2] = [(a, (0, 0)) for a in (low, high, low_other, high_other)]

    chosen, column = lax.optimization_barrier((chooser(channels, x), column))
    weights, table = in_order(chosen, ring_pieces(column, "x"))

    chips = 4 * ((y + jnp.arange(4)) % 4) + zl
    inside = jnp.stack([chips > 0, chips < 15], 1).astype(jnp.int32)
    flags = jnp.concatenate([core[None], inside.reshape(8)])
    results = {}
    for turn in (1, 2, 3, 0):
        done = mix(flags, parts[turn], weights, table, turn)
        if turn:
            done = lax.ppermute(done, "y", [(i, (i + turn) % 4) for i in range(4)])
        results[(4 - turn) % 4] = done
    keep = jnp.stack([results[i] for i in range(4)])
    give = jnp.stack([results[i][2:] for i in range(4)])
    take = lax.ppermute(give, "core", across)
    return weave(jnp.stack([core, y]), keep, take)


def solution(mesh):
    split = Mesh(mesh.devices.reshape(4, 4, 4, 4, 2), ("x", "zh", "y", "zl", "core"))
    img, band = ("x", "zh"), ("y", "zl", "core")
    placed = (
        P(img, band, None, None),
        P(img, band, None, None),
        P(img, band),
        P(band),
        P(None, band),
        P(band),
    )

    return jax.shard_map(
        on_device,
        mesh=split,
        in_specs=placed,
        out_specs=(P(img, band, None, None), P(img, band, None, None)),
        check_vma=False,
    )
```

```python
import functools

import jax
import jax.numpy as jnp
from jax import lax
from jax.experimental import pallas as pl
from jax.experimental.pallas import tpu as pltpu
from jax.sharding import Mesh
from jax.sharding import PartitionSpec as P


LANES = 128
DEPTH = 70
WIDTH = 176
HALF = WIDTH // 2
CORE = 64
REST = HALF - CORE
TAIL = 2 * REST
FOLD = DEPTH // 2
TABLE = DEPTH + FOLD
SPAN = 3
OUT_ROWS = 4
COLS = 64
GROUPS = 6


def ring_pieces(mine, axis):
    up = [(i, (i + 1) % 4) for i in range(4)]
    down = [((i + 1) % 4, i) for i in range(4)]
    cut = mine.shape[0] // 2
    before = lax.ppermute(mine, axis, up)
    after = lax.ppermute(mine, axis, down)
    low = lax.ppermute(before[:cut], axis, up)
    high = lax.ppermute(after[cut:], axis, down)
    return mine, after, low, high, before


def sigmoid(v):
    return 0.5 + 0.5 * jnp.tanh(0.5 * v)


def mix_kernel(flag_ref, *refs, slot):
    parts, (w_ref, table_ref, out_ref, x_ref, pre_ref, e_ref, m_ref) = refs[:4], refs[4:]
    core, first_in, last_in = flag_ref[0], flag_ref[1 + 2 * slot], flag_ref[2 + 2 * slot]
    n_part = 2 * SPAN * COLS
    for i, ref in enumerate(parts):
        x_ref[pl.ds(i * SPAN * COLS, SPAN * COLS), :] = ref[...].reshape(SPAN * COLS, -1)
    for n in range(GROUPS // 2):
        wide = jnp.dot(
            x_ref[...],
            w_ref[:, 2 * n * LANES : 2 * (n + 1) * LANES],
            preferred_element_type=jnp.float32,
        )
        pre_ref[2 * n] = wide[:, :LANES]
        pre_ref[2 * n + 1] = wide[:, LANES:]

    col = lax.broadcasted_iota(jnp.int32, (COLS, LANES), 0)
    lane = lax.broadcasted_iota(jnp.int32, (1, LANES), 1)

    def group(g, carry):
        bias, depth_bias = table_ref[g, pl.ds(9, 1), :], table_ref[g, pl.ds(10, 1), :]
        taps = [table_ref[g, pl.ds(i, 1), :] for i in range(9)]

        def act(r, inner):
            late = r // SPAN
            src = jnp.where(core == 0, late, 1 - late)
            at = pl.multiple_of(src * n_part + (r - SPAN * late) * COLS, COLS)
            p = pre_ref[g, pl.ds(at, COLS), :] + bias
            t = pre_ref[g, pl.ds(at + SPAN * COLS, COLS), :]
            sig = sigmoid(p)
            pair = (p * sig, sig * (1.0 + p * (1.0 - sig)) * t)
            last = jnp.where(r == 2 * SPAN - 1, last_in, 1)
            inside = jnp.where(r == 0, first_in, last) > 0
            for k in range(2):
                e = jnp.where(inside, pair[k].astype(jnp.bfloat16).astype(jnp.float32), 0.0)
                e_ref[k, 0, r] = jnp.where(col == 0, 0.0, pltpu.roll(e, 1, 0))
                e_ref[k, 1, r] = e
                e_ref[k, 2, r] = jnp.where(col == COLS - 1, 0.0, pltpu.roll(e, COLS - 1, 0))
            return inner

        def conv(q, inner):
            r = (2 * core + q) % OUT_ROWS
            for k in range(2):
                total = depth_bias if k == 0 else None
                for a in range(3):
                    for b in range(3):
                        term = e_ref[k, b, r + a] * taps[3 * a + b]
                        total = term if total is None else total + term
                m_ref[g, k, q] = total
            return inner

        lax.fori_loop(0, 2 * SPAN, act, 0, unroll=True)
        lax.fori_loop(0, OUT_ROWS, conv, 0, unroll=True)
        return carry

    lax.fori_loop(0, GROUPS, group, 0)

    def gated(q, to, split):
        (vp, gp), (vt, gt) = split(0), split(1)
        sig = sigmoid(gp)
        gate = gp * sig
        gate_t = sig * (1.0 + gp * (1.0 - sig)) * gt
        out_ref[q, to, 0] = (vp * gate).astype(jnp.bfloat16)
        out_ref[q, to, 1] = (vt * gate + vp * gate_t).astype(jnp.bfloat16)

    def rows(q, carry):
        for pair in range(2):

            def split(k, pair=pair):
                a, b = m_ref[2 * pair, k, q], m_ref[2 * pair + 1, k, q]
                value = jnp.where(lane < CORE, a, pltpu.roll(b, CORE, 1))
                return value, jnp.where(lane < CORE, pltpu.roll(a, CORE, 1), b)

            gated(q, pair, split)
        here = (lane < REST) | ((lane >= TAIL) & (lane < TAIL + REST))

        def split_tail(k):
            a, b = m_ref[4, k, q], m_ref[5, k, q]
            value = jnp.where(here, a, pltpu.roll(b, REST, 1))
            return value, jnp.where(here, pltpu.roll(a, LANES - REST, 1), b)

        gated(q, 2, split_tail)
        return carry

    lax.fori_loop(0, OUT_ROWS, rows, 0, unroll=True)


def mix(flags, parts, weights, table, slot):
    whole = pl.BlockSpec(memory_space=pltpu.VMEM)
    channels = weights.shape[0]

    def part(at):
        return pl.BlockSpec((1, 1, SPAN, COLS, channels), lambda i: (*at, 0, 0, 0))

    n_tok = 4 * SPAN * COLS
    return pl.pallas_call(
        functools.partial(mix_kernel, slot=slot),
        grid=(1,),
        out_shape=jax.ShapeDtypeStruct((OUT_ROWS, 3, 2, COLS, LANES), jnp.bfloat16),
        in_specs=[pl.BlockSpec(memory_space=pltpu.SMEM)] + [part(at) for _, at in parts] + [whole, whole],
        out_specs=whole,
        scratch_shapes=[
            pltpu.VMEM((n_tok, channels), jnp.bfloat16),
            pltpu.VMEM((GROUPS, n_tok, LANES), jnp.float32),
            pltpu.VMEM((2, 3, 2 * SPAN, COLS, LANES), jnp.float32),
            pltpu.VMEM((GROUPS, 2, OUT_ROWS, COLS, LANES), jnp.float32),
        ],
        cost_estimate=pl.CostEstimate(
            flops=2 * n_tok * weights.size, bytes_accessed=5_000_000, transcendentals=1_000_000
        ),
    )(flags, *[array for array, _ in parts], weights, table)


def order_kernel(x_ref, lines_ref, own, after, low, high, before, w_ref, table_ref):
    def block(j, zh, zl):
        if j == 2:
            return (low, 4 * zh + zl) if zh < 2 else (high, 4 * (zh - 2) + zl)
        return {0: own, 1: after, 3: before}[j], 4 * zh + zl

    lane = lax.broadcasted_iota(jnp.int32, (1, LANES), 1)

    def place(here):
        for xa in range(4):
            for zh in range(4):
                at = DEPTH * (4 * xa + zh)
                tails = []
                for zl in range(4):
                    ref, slot = block((xa - here) % 4, zh, zl)
                    whole = ref[slot].astype(jnp.float32)
                    w_ref[at : at + DEPTH, zl * LANES : (zl + 1) * LANES] = whole[:DEPTH].astype(
                        jnp.bfloat16
                    )
                    folded = whole[DEPTH:TABLE]
                    tails.append(
                        jnp.concatenate([folded, pltpu.roll(folded, LANES - TAIL, 1)], 0)
                    )
                for pair in range(2):
                    odd = jnp.where(lane < 2 * TAIL, pltpu.roll(tails[2 * pair + 1], TAIL, 1), 0.0)
                    w_ref[at : at + DEPTH, (4 + pair) * LANES : (5 + pair) * LANES] = jnp.where(
                        lane < TAIL, tails[2 * pair], odd
                    ).astype(jnp.bfloat16)

    for here in range(4):
        pl.when(x_ref[0] == here)(functools.partial(place, here))
    for i in range(11):
        at, row = 4 * (i // 3), i % 3
        line = lambda zl, r: lines_ref[at + zl, pl.ds(r, 1), :]
        for zl in range(4):
            table_ref[zl, pl.ds(i, 1), :] = line(zl, row)
        for pair in range(2):
            odd = jnp.where(lane < 2 * TAIL, pltpu.roll(line(2 * pair + 1, row + 3), TAIL, 1), 0.0)
            table_ref[4 + pair, pl.ds(i, 1), :] = jnp.where(lane < TAIL, line(2 * pair, row + 3), odd)


def in_order(x, lines, pieces):
    whole = pl.BlockSpec(memory_space=pltpu.VMEM)
    channels = 16 * DEPTH
    return pl.pallas_call(
        order_kernel,
        out_shape=(
            jax.ShapeDtypeStruct((channels, GROUPS * LANES), jnp.bfloat16),
            jax.ShapeDtypeStruct((GROUPS, 12, LANES), jnp.float32),
        ),
        in_specs=[pl.BlockSpec(memory_space=pltpu.SMEM)] + [whole] * 6,
        out_specs=(whole, whole),
        cost_estimate=pl.CostEstimate(flops=10_000_000, bytes_accessed=4_000_000, transcendentals=0),
    )(x[None], lines, *pieces)


def weave_kernel(flag_ref, keep_ref, take_ref, *out):
    mine_first = flag_ref[0] == 0
    y = flag_ref[1]
    lane = lax.broadcasted_iota(jnp.int32, (1, LANES), 1)

    def row(r, carry):
        for k in range(2):
            segments = []
            for source in range(4):
                at = (source - y + 4) % 4
                groups = []
                for g in range(3):
                    own = keep_ref[at, r, g, k].astype(jnp.float32)
                    other = take_ref[at, r, g, k].astype(jnp.float32)
                    groups.append(
                        (jnp.where(mine_first, own, other), jnp.where(mine_first, other, own))
                    )
                for zl in range(4):
                    for core in range(2):
                        start = WIDTH * (8 * (source % 2) + 2 * zl + core) + HALF * (source // 2)
                        odd, pair = zl % 2, zl // 2
                        segments.append((start, CORE * odd, CORE, groups[pair][core]))
                        lanes = TAIL * odd + REST * pair
                        segments.append((start + CORE, lanes, REST, groups[2][core]))
            for n in range(16 * WIDTH // LANES):
                tile = None
                for start, first, count, block in segments:
                    lo, hi = start - n * LANES, start + count - n * LANES
                    if hi <= 0 or lo >= LANES:
                        continue
                    shift = (lo - first) % LANES
                    moved = pltpu.roll(block, shift, 1) if shift else block
                    if tile is None:
                        tile = moved
                    else:
                        tile = jnp.where((lane >= lo) & (lane < hi), moved, tile)
                out[k][0, r, :, pl.ds(n * LANES, LANES)] = tile.astype(jnp.bfloat16)
        return carry

    lax.fori_loop(0, 2, row, 0)


def weave(flags, keep, take):
    out = jax.ShapeDtypeStruct((1, 2, COLS, 16 * WIDTH), jnp.bfloat16)
    whole = pl.BlockSpec(memory_space=pltpu.VMEM)
    return pl.pallas_call(
        weave_kernel,
        out_shape=(out, out),
        in_specs=[pl.BlockSpec(memory_space=pltpu.SMEM)] + [whole] * 2,
        out_specs=(whole, whole),
    )(flags, keep, take)


def on_device(latents, tangents, w_expand, b_expand, w_depth, b_depth):
    core, x, y = lax.axis_index("core"), lax.axis_index("x"), lax.axis_index("y")
    zl = lax.axis_index("zl")
    across = [(0, 1), (1, 0)]
    small = jnp.concatenate([w_depth, b_expand[None], b_depth[None], jnp.zeros_like(b_depth)[None]], 0)
    three = lax.dynamic_slice_in_dim(small, 3 * lax.axis_index("zh"), 3, 0)
    shard = jnp.concatenate([w_expand, three], 0)
    front = y < 2
    low, high = shard[:, :HALF], shard[:, HALF:]
    got = lax.ppermute(jnp.where(front, high, low), "y", [(i, (i + 2) % 4) for i in range(4)])
    held = jnp.where(front, low, high)
    value, gate = jnp.where(front, held, got), jnp.where(front, got, held)
    zeros = lambda rows, lanes: jnp.zeros((rows, lanes), w_expand.dtype)
    main = jnp.concatenate([value[:, :CORE], gate[:, :CORE]], 1)
    tail = jnp.concatenate([value[:, CORE:], gate[:, CORE:]], 1)
    block = jnp.concatenate(
        [
            main[:DEPTH],
            jnp.concatenate([tail[:FOLD], tail[FOLD:DEPTH], zeros(FOLD, LANES - 2 * TAIL)], 1),
            main[DEPTH:],
            jnp.concatenate([tail[DEPTH:], zeros(3, LANES - TAIL)], 1),
            zeros(1, LANES),
        ],
        0,
    )
    sent = jnp.broadcast_to(block[None], (16,) + block.shape)

    edge = jnp.where(
        core == 0,
        jnp.concatenate([latents[:, 0], tangents[:, 0]], 0),
        jnp.concatenate([latents[:, -1], tangents[:, -1]], 0),
    )
    near = [(2 * q + 1, 2 * q + 2) for q in range(15)]
    beyond = lax.ppermute(edge, ("y", "zl", "core"), near + [(b, a) for a, b in near])
    rows = [jnp.concatenate([latents[:, r], tangents[:, r]], 0) for r in range(2)]
    mine = jnp.stack(
        [
            jnp.where(core == 0, beyond, rows[0]),
            jnp.where(core == 0, rows[0], rows[1]),
            jnp.where(core == 0, rows[1], beyond),
        ],
        1,
    )
    sent, mine = lax.optimization_barrier((sent, mine))
    column = lax.all_to_all(sent, ("zh", "zl"), 0, 0)
    own, after, low, high, before = ring_pieces(mine, "y")
    near = jnp.stack([own, after, before])
    low, high = low[None], high[None]
    near_other = lax.ppermute(near, "core", across)
    low_other = lax.ppermute(low, "core", across)
    high_other = lax.ppermute(high, "core", across)
    parts = {
        i: [(near, (at, 0)), (near, (at, 1)), (near_other, (at, 0)), (near_other, (at, 1))]
        for i, at in ((0, 0), (1, 1), (3, 2))
    }
    parts[2] = [(a, (0, 0)) for a in (low, high, low_other, high_other)]

    lines = column[:, TABLE : TABLE + 6].astype(jnp.float32)
    weights, table = in_order(x, lines, ring_pieces(column, "x"))

    chips = 4 * ((y + jnp.arange(4)) % 4) + zl
    inside = jnp.stack([chips > 0, chips < 15], 1).astype(jnp.int32)
    flags = jnp.concatenate([core[None], inside.reshape(8)])
    results = {}
    for turn in (1, 2, 3, 0):
        done = mix(flags, parts[turn], weights, table, turn)
        if turn:
            done = lax.ppermute(done, "y", [(i, (i + turn) % 4) for i in range(4)])
        results[(4 - turn) % 4] = done
    keep = jnp.stack([results[i] for i in range(4)])
    give = jnp.stack([results[i][2:] for i in range(4)])
    take = lax.ppermute(give, "core", across)
    return weave(jnp.stack([core, y]), keep, take)


def solution(mesh):
    split = Mesh(mesh.devices.reshape(4, 4, 4, 4, 2), ("x", "zh", "y", "zl", "core"))
    img, band = ("x", "zh"), ("y", "zl", "core")
    placed = (
        P(img, band, None, None),
        P(img, band, None, None),
        P(img, band),
        P(band),
        P(None, band),
        P(band),
    )

    return jax.shard_map(
        on_device,
        mesh=split,
        in_specs=placed,
        out_specs=(P(img, band, None, None), P(img, band, None, None)),
        check_vma=False,
    )
```
